32 devices in a mesh: dp: 4 (over y, core), px: 2 (over x), py: 4 (over z).
Axes of the slice: x: 2, y: 2, z: 4, core: 2. Of those that a mesh axis runs over, the one named last changes fastest.
Arguments:
- state_a: bfloat16 [4, 16, 128, 128, 128], P('dp', None, 'px', 'py'), may hold values from -6 to 6
- state_b: bfloat16 [4, 16, 128, 128, 128], P('dp', None, 'px', 'py'), may hold values from -6 to 6
- cotan_a: bfloat16 [4, 16, 128, 128, 128], P('dp', None, 'px', 'py'), may hold values from -6 to 6
- cotan_b: bfloat16 [4, 16, 128, 128, 128], P('dp', None, 'px', 'py'), may hold values from -6 to 6
- spectral_weight: bfloat16 [32, 8, 32, 2, 16, 16], P('py', None, 'px'), may hold values from -1 to 1
- point_weight: bfloat16 [16, 16], replicated, may hold values from -1.5 to 1.5
Outputs:
- input_a: bfloat16 [4, 16, 128, 128, 128], P('dp', None, 'px', 'py')
- grad_b: bfloat16 [4, 16, 128, 128, 128], P('dp', None, 'px', 'py')
- spectral_grad: float32 [32, 8, 32, 2, 16, 16], P('py', None, 'px', None, None, 'dp')
- point_grad: float32 [16, 16], replicated
The draws below stay inside these ranges and needn't reach their ends.
All inputs are finite; a program needn't handle non-finite values.
Results may differ from the reference program's by a relative error of at most 0.0038.
Values sent between devices are 32-bit elements; how exact they have to be, the bound alone decides.
A program may use at most 384 MiB of HBM per device.

```python
import math
import jax
import jax.numpy as jnp
from jax import lax

CH = 16
NX = 128
NY = 128
NZ = 128
MX = 32
MY = 32
MZ = 8
BATCH = 4


def block_levels(own_key, extent, split, smallest, largest):
    loudness, own = 1.0, jax.random.fold_in(own_key, 6)
    for position, parts in split:
        steps = jnp.exp(jax.random.uniform(jax.random.fold_in(own, position), (parts,), jnp.float32, smallest / len(split), largest / len(split)))
        loudness = loudness * jnp.repeat(steps, extent[position] // parts).reshape([-1 if axis == position else 1 for axis in range(len(extent))])
    return loudness


def bell_draw(rng, extent, deviation, most, cuts=(), kind=jnp.bfloat16):
    level = block_levels(rng, extent, cuts, -0.22, 0.18) if cuts else 1.0
    result = jax.random.normal(rng, extent, jnp.float32) * deviation * level
    return jnp.minimum(jnp.maximum(result, -most), most).astype(kind)


def setup_inputs(seed: int = 0) -> dict:
    streams_of = jax.random.split(jax.random.key(seed), 7)
    return {
        "state_a": bell_draw(streams_of[0], (BATCH, CH, NY, NZ, NX), 1.0, 6.0, ((0, 4), (2, 2), (3, 4))),
        "state_b": bell_draw(streams_of[1], (BATCH, CH, NY, NZ, NX), 1.0, 6.0, ((0, 4), (2, 2), (3, 4))),
        "cotan_a": bell_draw(streams_of[2], (BATCH, CH, NY, NZ, NX), 1.0, 6.0, ((0, 4), (2, 2), (3, 4))),
        "cotan_b": bell_draw(streams_of[3], (BATCH, CH, NY, NZ, NX), 1.0, 6.0, ((0, 4), (2, 2), (3, 4))),
        "spectral_weight": bell_draw(streams_of[4], (MY, MZ, MX, 2, CH, CH), (2 * CH) ** -0.5, 1.0, ((0, 4), (2, 2))),
        "point_weight": bell_draw(streams_of[5], (CH, CH), CH ** -0.5, 1.5),
    }


HIGHEST = lax.Precision.HIGHEST

def kept_frequencies(length_all, length_kept):
    positions = jnp.arange(length_kept, dtype=jnp.int32)
    return jnp.where(positions < length_kept // 2, positions, length_all - length_kept + positions).astype(jnp.int32)

def forward_plain(field_in):
    along_x = jnp.fft.fft(field_in, axis=3)[:, :, :, :MX]
    along_y = jnp.take(jnp.fft.fft(along_x, axis=1), kept_frequencies(NY, MY), axis=1)
    along_z = jnp.take(jnp.fft.fft(along_y, axis=2), kept_frequencies(NZ, MZ), axis=2)
    return jnp.stack([jnp.real(along_z), jnp.imag(along_z)], axis=3)

def inverse_plain(spectrum):
    values = spectrum[:, :, :, 0] + 1j * spectrum[:, :, :, 1]
    chans = values.shape[0]
    full_z = jnp.zeros((chans, MY, NZ, MX), values.dtype).at[:, :, kept_frequencies(NZ, MZ)].set(values)
    back_z = jnp.fft.ifft(full_z, axis=2) * NZ
    full_y = jnp.zeros((chans, NY, NZ, MX), values.dtype).at[:, kept_frequencies(NY, MY)].set(back_z)
    back_y = jnp.fft.ifft(full_y, axis=1) * NY
    full_x = jnp.zeros((chans, NY, NZ, NX), values.dtype).at[:, :, :, :MX].set(back_y)
    return jnp.real(jnp.fft.ifft(full_x, axis=3)) * NX

def spectral_product(spectrum, weight):
    pattern = 'cjlk,jlkcd->djlk'
    real_in = spectrum[:, :, :, 0]
    imag_in = spectrum[:, :, :, 1]
    w_real = weight[:, :, :, 0]
    w_imag = weight[:, :, :, 1]
    out_real = jnp.einsum(pattern, real_in, w_real, precision=HIGHEST) - jnp.einsum(pattern, imag_in, w_imag, precision=HIGHEST)
    out_imag = jnp.einsum(pattern, real_in, w_imag, precision=HIGHEST) + jnp.einsum(pattern, imag_in, w_real, precision=HIGHEST)
    return jnp.stack([out_real, out_imag], axis=3)

def spectral_adjoint(back_spec, weight):
    pattern = 'djlk,jlkcd->cjlk'
    real_in = back_spec[:, :, :, 0]
    imag_in = back_spec[:, :, :, 1]
    w_real = weight[:, :, :, 0]
    w_imag = weight[:, :, :, 1]
    out_real = jnp.einsum(pattern, real_in, w_real, precision=HIGHEST) + jnp.einsum(pattern, imag_in, w_imag, precision=HIGHEST)
    out_imag = jnp.einsum(pattern, imag_in, w_real, precision=HIGHEST) - jnp.einsum(pattern, real_in, w_imag, precision=HIGHEST)
    return jnp.stack([out_real, out_imag], axis=3)

def spectral_outer(spectrum, back_spec):
    pattern = 'cjlk,djlk->jlkcd'
    spec_real = spectrum[:, :, :, 0]
    spec_imag = spectrum[:, :, :, 1]
    back_real = back_spec[:, :, :, 0]
    back_imag = back_spec[:, :, :, 1]
    grad_real = jnp.einsum(pattern, spec_real, back_real, precision=HIGHEST) + jnp.einsum(pattern, spec_imag, back_imag, precision=HIGHEST)
    grad_imag = jnp.einsum(pattern, spec_real, back_imag, precision=HIGHEST) - jnp.einsum(pattern, spec_imag, back_real, precision=HIGHEST)
    return jnp.stack([grad_real, grad_imag], axis=3)

def reference(state_a, state_b, cotan_a, cotan_b, spectral_weight, point_weight):
    samples = state_a.shape[0]
    scale_f = 1.0 / math.sqrt(NX * NY * NZ)
    scale_i = 1.0 / math.sqrt(MX * MY * MZ)
    grad_scale = math.sqrt(MX * MY * MZ / (samples * NX * NY * NZ))
    point_scale = 1.0 / math.sqrt(samples * NX * NY * NZ)
    weight = spectral_weight.astype(jnp.float32)
    pointwise = point_weight.astype(jnp.float32)
    rebuilt = []
    grads_second = []
    spectral_total = jnp.zeros(spectral_weight.shape, jnp.float32)
    point_total = jnp.zeros(point_weight.shape, jnp.float32)
    for sample in range(samples):
        field_wide = state_b[sample].astype(jnp.float32)
        spectrum = forward_plain(field_wide) * scale_f
        mixed_spec = spectral_product(spectrum, weight)
        local_point = jnp.einsum('cyzn,cd->dyzn', field_wide, pointwise, precision=HIGHEST)
        hidden = inverse_plain(mixed_spec) * scale_i + local_point
        activated, pullback = jax.vjp(jax.nn.gelu, hidden)
        rebuilt.append((state_a[sample].astype(jnp.float32) - activated).astype(jnp.bfloat16))
        slope_grad = pullback(cotan_a[sample].astype(jnp.float32))[0].astype(jnp.bfloat16)
        slope_wide = slope_grad.astype(jnp.float32)
        back_spec = forward_plain(slope_wide) * scale_i
        spectral_total = spectral_total + spectral_outer(spectrum, back_spec)
        spec_grad = spectral_adjoint(back_spec, weight)
        point_back = jnp.einsum('dyzn,cd->cyzn', slope_wide, pointwise, precision=HIGHEST)
        second = cotan_b[sample].astype(jnp.float32) + inverse_plain(spec_grad) * scale_f + point_back
        grads_second.append(second.astype(jnp.bfloat16))
        point_total = point_total + jnp.einsum('cyzn,dyzn->cd', field_wide, slope_wide, precision=HIGHEST)
    return (jnp.stack(rebuilt), jnp.stack(grads_second), spectral_total * grad_scale, point_total * point_scale)
```

```python
import math

import jax
import jax.numpy as jnp
import numpy as np
from jax import lax
from jax.experimental import pallas as pl
from jax.experimental.pallas import tpu as pltpu
from jax.sharding import PartitionSpec as P

MX = 32
MY = 32
MZ = 8
GROUP = 4
SUB = 16
LIMIT = 56 * 1024 * 1024
INTERPRET = False
F32 = jnp.float32
BF16 = jnp.bfloat16


def kept(length_all, length_kept, position):
    return jnp.where(position < length_kept // 2, position, length_all - length_kept + position)


def angle(product, length_all):
    return (product % length_all).astype(F32) * (2.0 * math.pi / length_all)


def split(value):
    high = lax.reduce_precision(value, 8, 7)
    return high.astype(BF16), (value - high).astype(BF16)


def synthesis_table(shape):
    ys, zs, ny, nz = shape
    mode = lax.broadcasted_iota(jnp.int32, (1, MY * MZ), 1)
    fy = kept(ny, MY, mode // MZ)
    fz = kept(nz, MZ, mode % MZ)
    y = lax.axis_index("px") * ys + lax.broadcasted_iota(jnp.int32, (ys, 1), 0)
    z = lax.axis_index("py") * zs + lax.broadcasted_iota(jnp.int32, (zs, 1), 0)
    ay = angle(fy * y, ny)
    az = angle(fz * z, nz)
    cy, sy = jnp.cos(ay)[:, None, :], jnp.sin(ay)[:, None, :]
    cz, sz = jnp.cos(az)[None], jnp.sin(az)[None]
    table = jnp.concatenate([cy * cz - sy * sz, -(sy * cz + cy * sz)], axis=2)
    return table.reshape(ys * zs, 2 * MY * MZ)


def analysis_table(shape):
    ys, zs, ny, nz = shape
    cell = lax.broadcasted_iota(jnp.int32, (1, ys * zs), 1)
    y = lax.axis_index("px") * ys + cell // zs
    z = lax.axis_index("py") * zs + cell % zs
    fy = kept(ny, MY, lax.broadcasted_iota(jnp.int32, (MY, 1), 0))
    fz = kept(nz, MZ, lax.broadcasted_iota(jnp.int32, (MZ, 1), 0))
    ay = angle(fy * y, ny)
    az = angle(fz * z, nz)
    cy, sy = jnp.cos(ay)[:, None, :], jnp.sin(ay)[:, None, :]
    cz, sz = jnp.cos(az)[None], jnp.sin(az)[None]
    table = jnp.stack([cy * cz - sy * sz, -(sy * cz + cy * sz)])
    return table.reshape(2 * MY * MZ, ys * zs)


def x_tables(px, nx):
    kk = MX // px
    k = np.arange(MX).reshape(px, kk)
    phase = 2.0 * np.pi / nx * (k[:, :, None] * np.arange(nx) % nx)
    cosine, sine = np.cos(phase), np.sin(phase)
    table = np.zeros((2, px, GROUP, 2, kk, GROUP, nx))
    for c in range(GROUP):
        table[0, :, c, 0, :, c] = cosine
        table[0, :, c, 1, :, c] = -sine
        table[1, :, c, 0, :, c] = sine
        table[1, :, c, 1, :, c] = cosine
    table = table.reshape(2, 2 * MX * GROUP, GROUP * nx)
    high = table.astype(BF16)
    low = (table - high.astype(np.float64)).astype(BF16)
    return high, low


def dot(a, b):
    return jnp.dot(a, b, preferred_element_type=F32)


def cut(value):
    high = value.astype(BF16)
    return high, (value - high.astype(F32)).astype(BF16)


def dot3(a, high, low):
    ahigh, alow = cut(a)
    return dot(ahigh, high) + dot(alow, high) + dot(ahigh, low)


def to_modes(b0, b1, xh_ref, xl_ref):
    return dot3(b0, xh_ref[0], xl_ref[0]) + dot3(b1, xh_ref[1], xl_ref[1])


def store_modes(out_ref, group, value, px, py):
    wide = value.shape[1] // px
    tall = value.shape[0] // py
    for i in range(px):
        for j in range(py):
            out_ref[i * py + j, group] = value[j * tall : (j + 1) * tall, i * wide : (i + 1) * wide]


def build_fields(spec_ref, xh_ref, xl_ref, gh_ref, gl_ref, px, py):
    modes = MY * MZ
    for g in range(spec_ref.shape[1]):
        rows = []
        for j in range(py):
            rows.append(jnp.concatenate([spec_ref[i * py + j, g] for i in range(px)], axis=1))
        value = jnp.concatenate(rows, axis=0)
        for t in range(2):
            high, low = cut(dot3(value, xh_ref[t], xl_ref[t]))
            half = high.shape[1] // 2
            for h in range(2):
                gh_ref[2 * g + h, t * modes : (t + 1) * modes] = high[:, h * half : (h + 1) * half]
                gl_ref[2 * g + h, t * modes : (t + 1) * modes] = low[:, h * half : (h + 1) * half]


def pair_of(ref, start):
    chans, _, nx = ref.shape
    first = ref[:, pl.ds(start, SUB), :].reshape(chans * SUB, nx)
    second = ref[:, pl.ds(start + SUB, SUB), :].reshape(chans * SUB, nx)
    return jnp.concatenate([first, second], axis=1)


def channel_mix(kron_ref, in_ref, out_ref):
    chans, rows, nx = in_ref.shape

    def body(q, carry):
        start = pl.multiple_of(q * 2 * SUB, 2 * SUB)
        value = dot(kron_ref[...], pair_of(in_ref, start))
        out_ref[:, pl.ds(start, SUB), :] = value[:, :nx].reshape(chans, SUB, nx)
        out_ref[:, pl.ds(start + SUB, SUB), :] = value[:, nx:].reshape(chans, SUB, nx)
        return carry

    lax.fori_loop(0, rows // (2 * SUB), body, 0)


def forward_kernel(px, py, v_ref, th_ref, tl_ref, xh_ref, xl_ref, out_ref):
    modes = MY * MZ
    parts = []
    for p in range(GROUP // 2):
        value = jnp.concatenate([v_ref[2 * p], v_ref[2 * p + 1]], axis=1)
        parts.append(dot(th_ref[...], value) + dot(tl_ref[...], value))
    b0 = jnp.concatenate([part[:modes] for part in parts], axis=1)
    b1 = jnp.concatenate([part[modes:] for part in parts], axis=1)
    store_modes(out_ref, 0, to_modes(b0, b1, xh_ref, xl_ref), px, py)


def middle_kernel(
    px, py, steps, spec_ref, vb_ref, va_ref, ca_ref, uh_ref, ul_ref, th_ref, tl_ref, xh_ref, xl_ref, fh_ref, fl_ref,
    kron_ref, ia_ref, sl_ref, back_ref, point_ref, gh_ref, gl_ref, acc_ref, mix_ref,
):
    step = pl.program_id(0)
    modes = MY * MZ
    nx = vb_ref.shape[2]
    chans, rows = vb_ref.shape[:2]

    @pl.when(step == 0)
    def _():
        build_fields(spec_ref, xh_ref, xl_ref, gh_ref, gl_ref, px, py)
        acc_ref[...] = jnp.zeros_like(acc_ref)
        point_ref[...] = jnp.zeros_like(point_ref)

    channel_mix(kron_ref, vb_ref, mix_ref)
    c0 = math.sqrt(2.0 / math.pi)

    def body(p, carry):
        field = dot(uh_ref[...], gh_ref[p]) + dot(ul_ref[...], gh_ref[p]) + dot(uh_ref[...], gl_ref[p])
        slopes = []
        for h in range(2):
            d = 2 * p + h
            v = field[:, h * nx : (h + 1) * nx] + mix_ref[d]
            v2 = v * v
            t = jnp.tanh(v * (c0 + (c0 * 0.044715) * v2))
            half = 0.5 + 0.5 * t
            ia_ref[d] = (va_ref[d].astype(F32) - v * half).astype(BF16)
            deriv = half + (0.5 * v) * (1.0 - t * t) * (c0 + (3.0 * c0 * 0.044715) * v2)
            slope = (ca_ref[d].astype(F32) * deriv).astype(BF16)
            sl_ref[d] = slope
            slopes.append(slope)
        both = jnp.concatenate(slopes, axis=1)
        acc_ref[p] += dot(th_ref[...], both) + dot(tl_ref[...], both)
        return carry

    lax.fori_loop(0, chans // 2, body, 0)

    def point_body(q, carry):
        start = pl.multiple_of(q * 2 * SUB, 2 * SUB)
        point_ref[...] += lax.dot_general(
            pair_of(vb_ref, start), pair_of(sl_ref, start), (((1,), (1,)), ((), ())), preferred_element_type=F32
        )
        return carry

    lax.fori_loop(0, rows // (2 * SUB), point_body, 0)

    @pl.when(step == steps - 1)
    def _():
        for g in range(chans // GROUP):
            parts = [acc_ref[2 * g + h] for h in range(2)]
            b0 = jnp.concatenate([part[:modes] for part in parts], axis=1)
            b1 = jnp.concatenate([part[modes:] for part in parts], axis=1)
            store_modes(back_ref, g, to_modes(b0, b1, fh_ref, fl_ref), px, py)


def last_kernel(
    px, py, spec_ref, sl_ref, cb_ref, uh_ref, ul_ref, xh_ref, xl_ref, kron_ref, out_ref, gh_ref, gl_ref, mix_ref
):
    nx = sl_ref.shape[2]

    @pl.when(pl.program_id(0) == 0)
    def _():
        build_fields(spec_ref, xh_ref, xl_ref, gh_ref, gl_ref, px, py)

    channel_mix(kron_ref, sl_ref, mix_ref)

    def body(p, carry):
        field = dot(uh_ref[...], gh_ref[p]) + dot(ul_ref[...], gh_ref[p]) + dot(uh_ref[...], gl_ref[p])
        for h in range(2):
            d = 2 * p + h
            value = cb_ref[d].astype(F32) + field[:, h * nx : (h + 1) * nx] + mix_ref[d]
            out_ref[d] = value.astype(BF16)
        return carry

    lax.fori_loop(0, sl_ref.shape[0] // 2, body, 0)


def whole(shape):
    return pl.BlockSpec(shape, lambda i: (0,) * len(shape), pipeline_mode=pl.Buffered(1))


def per_device(state_a, state_b, cotan_a, cotan_b, spectral_weight, point_weight):
    samples, px, py = (lax.axis_size(name) for name in ("dp", "px", "py"))
    _, chans, ys, zs, nx = state_b.shape
    ny, nz = ys * px, zs * py
    cells, modes = ys * zs, MY * MZ
    groups = chans // GROUP
    kk = MX // px
    tall, wide = modes // py, 2 * MX * GROUP // px
    own = tall * kk
    scale_f = 1.0 / math.sqrt(nx * ny * nz)
    scale_i = 1.0 / math.sqrt(MX * MY * MZ)
    grad_scale = math.sqrt(MX * MY * MZ / (samples * nx * ny * nz))
    point_scale = 1.0 / math.sqrt(samples * nx * ny * nz)
    shape = (ys, zs, ny, nz)
    th, tl = split(analysis_table(shape))
    uh, ul = split(synthesis_table(shape))
    xh, xl = x_tables(px, nx)
    fh, fl = (jnp.asarray(np.ascontiguousarray(table.transpose(0, 2, 1))) for table in (xh, xl))
    xh, xl = jnp.asarray(xh), jnp.asarray(xl)
    eye = jnp.eye(SUB, dtype=BF16)
    kron_f = (point_weight.T[:, None, :, None] * eye[None, :, None, :]).reshape(chans * SUB, chans * SUB)
    kron_b = (point_weight[:, None, :, None] * eye[None, :, None, :]).reshape(chans * SUB, chans * SUB)
    field_a, field_b, cot_a, cot_b = (
        value.reshape(chans, cells, nx) for value in (state_a, state_b, cotan_a, cotan_b)
    )
    part_shape = jax.ShapeDtypeStruct((px * py, groups, tall, wide), F32)
    params = pltpu.CompilerParams(vmem_limit_bytes=LIMIT)

    part = pl.pallas_call(
        lambda *refs: forward_kernel(px, py, *refs),
        grid=(groups,),
        in_specs=[
            pl.BlockSpec((GROUP, cells, nx), lambda i: (i, 0, 0)),
            whole(th.shape), whole(tl.shape), whole(fh.shape), whole(fl.shape),
        ],
        out_specs=pl.BlockSpec((px * py, 1, tall, wide), lambda i: (0, i, 0, 0)),
        out_shape=part_shape,
        compiler_params=params,
        interpret=INTERPRET,
        name="forward",
    )(field_b, th, tl, fh, fl)

    def scatter(value):
        value = lax.psum_scatter(value, ("px", "py"), scatter_dimension=0, tiled=True)
        value = value.reshape(groups, tall, GROUP, 2, kk).transpose(3, 0, 2, 1, 4)
        return value.reshape(2, chans, own)

    def gather(real, imag):
        value = jnp.stack([real, imag]).reshape(2, groups, GROUP, tall, kk).transpose(1, 3, 2, 0, 4)
        value = value.reshape(1, groups, tall, wide)
        return lax.all_gather(value, ("px", "py"), axis=0, tiled=True)

    weight = spectral_weight.transpose(3, 4, 5, 0, 1, 2).reshape(2, chans, chans, own).astype(F32)
    w_real, w_imag = weight[0], weight[1]
    spectrum = scatter(part) * scale_f
    s_real, s_imag = spectrum[0][:, None], spectrum[1][:, None]
    mixed = gather(
        jnp.sum(s_real * w_real - s_imag * w_imag, axis=0) * scale_i,
        jnp.sum(s_real * w_imag + s_imag * w_real, axis=0) * scale_i,
    )

    rows = min(256, cells)
    steps = cells // rows
    block = pl.BlockSpec((chans, rows, nx), lambda i: (0, i, 0))
    u_block = pl.BlockSpec((rows, 2 * modes), lambda i: (i, 0))
    t_block = pl.BlockSpec((2 * modes, rows), lambda i: (0, i))
    field_shape = jax.ShapeDtypeStruct((chans, cells, nx), BF16)
    side = chans * SUB
    g_scratch = [pltpu.VMEM((chans // 2, 2 * modes, 2 * nx), BF16)] * 2
    input_a, slope, back_part, point = pl.pallas_call(
        lambda *refs: middle_kernel(px, py, steps, *refs),
        grid=(steps,),
        in_specs=[
            whole(part_shape.shape), block, block, block, u_block, u_block, t_block, t_block,
            whole(xh.shape), whole(xl.shape), whole(fh.shape), whole(fl.shape), whole((side, side)),
        ],
        out_specs=[block, block, whole(part_shape.shape), whole((side, side))],
        out_shape=[field_shape, field_shape, part_shape, jax.ShapeDtypeStruct((side, side), F32)],
        scratch_shapes=g_scratch
        + [pltpu.VMEM((chans // 2, 2 * modes, 2 * nx), F32), pltpu.VMEM((chans, rows, nx), F32)],
        compiler_params=params,
        interpret=INTERPRET,
        name="middle",
    )(mixed, field_b, field_a, cot_a, uh, ul, th, tl, xh, xl, fh, fl, kron_f)

    back = scatter(back_part) * scale_i
    b_real, b_imag = back[0][None], back[1][None]
    grad_spec = gather(
        jnp.sum(b_real * w_real + b_imag * w_imag, axis=1) * scale_f,
        jnp.sum(b_imag * w_real - b_real * w_imag, axis=1) * scale_f,
    )
    grad_b = pl.pallas_call(
        lambda *refs: last_kernel(px, py, *refs),
        grid=(steps,),
        in_specs=[
            whole(part_shape.shape), block, block, u_block, u_block,
            whole(xh.shape), whole(xl.shape), whole((side, side)),
        ],
        out_specs=block,
        out_shape=field_shape,
        scratch_shapes=g_scratch + [pltpu.VMEM((chans, rows, nx), F32)],
        compiler_params=params,
        interpret=INTERPRET,
        name="last",
    )(grad_spec, slope, cot_b, uh, ul, xh, xl, kron_b)

    share = chans // samples
    spec_all = lax.all_gather(spectrum, "dp", axis=0)
    back_all = lax.all_gather(back, "dp", axis=0)
    back_own = lax.dynamic_slice_in_dim(back_all, lax.axis_index("dp") * share, share, axis=2)
    p_real, p_imag = spec_all[:, 0, :, None], spec_all[:, 1, :, None]
    q_real, q_imag = back_own[:, 0, None], back_own[:, 1, None]
    grad_real = jnp.sum(p_real * q_real + p_imag * q_imag, axis=0)
    grad_imag = jnp.sum(p_real * q_imag - p_imag * q_real, axis=0)
    grad = jnp.stack([grad_real, grad_imag]) * grad_scale
    spectral_grad = grad.reshape(2, chans, share, tall // MZ, MZ, kk).transpose(3, 4, 5, 0, 1, 2)

    point = jnp.sum(point.reshape(chans, SUB, chans, SUB) * jnp.eye(SUB, dtype=F32)[None, :, None, :], axis=(1, 3))
    point_total = lax.psum(point, ("dp", "px", "py")) * point_scale
    full = state_b.shape
    return (input_a.reshape(full), grad_b.reshape(full), spectral_grad, point_total)


def solution(mesh):
    return jax.shard_map(
        per_device,
        mesh=mesh,
        in_specs=(
            P("dp", None, "px", "py", None),
            P("dp", None, "px", "py", None),
            P("dp", None, "px", "py", None),
            P("dp", None, "px", "py", None),
            P("py", None, "px", None, None, None),
            P(),
        ),
        out_specs=(
            P("dp", None, "px", "py", None),
            P("dp", None, "px", "py", None),
            P("py", None, "px", None, None, "dp"),
            P(),
        ),
        check_vma=False,
    )
```

```python
import math

import jax
import jax.numpy as jnp
import numpy as np
from jax import lax
from jax.experimental import pallas as pl
from jax.experimental.pallas import tpu as pltpu
from jax.sharding import PartitionSpec as P

MX = 32
MY = 32
MZ = 8
GROUP = 4
SUB = 16
LIMIT = 56 * 1024 * 1024
INTERPRET = False
F32 = jnp.float32
BF16 = jnp.bfloat16


def kept(length_all, length_kept, position):
    return jnp.where(position < length_kept // 2, position, length_all - length_kept + position)


def angle(product, length_all):
    return (product % length_all).astype(F32) * (2.0 * math.pi / length_all)


def synthesis_table(shape):
    ys, zs, ny, nz = shape
    mode = lax.broadcasted_iota(jnp.int32, (1, MY * MZ), 1)
    fy = kept(ny, MY, mode // MZ)
    fz = kept(nz, MZ, mode % MZ)
    y = lax.axis_index("px") * ys + lax.broadcasted_iota(jnp.int32, (ys, 1), 0)
    z = lax.axis_index("py") * zs + lax.broadcasted_iota(jnp.int32, (zs, 1), 0)
    ay = angle(fy * y, ny)
    az = angle(fz * z, nz)
    cy, sy = jnp.cos(ay)[:, None, :], jnp.sin(ay)[:, None, :]
    cz, sz = jnp.cos(az)[None], jnp.sin(az)[None]
    table = jnp.concatenate([cy * cz - sy * sz, -(sy * cz + cy * sz)], axis=2)
    return table.reshape(ys * zs, 2 * MY * MZ)


def analysis_table(shape):
    ys, zs, ny, nz = shape
    cell = lax.broadcasted_iota(jnp.int32, (1, ys * zs), 1)
    y = lax.axis_index("px") * ys + cell // zs
    z = lax.axis_index("py") * zs + cell % zs
    fy = kept(ny, MY, lax.broadcasted_iota(jnp.int32, (MY, 1), 0))
    fz = kept(nz, MZ, lax.broadcasted_iota(jnp.int32, (MZ, 1), 0))
    ay = angle(fy * y, ny)
    az = angle(fz * z, nz)
    cy, sy = jnp.cos(ay)[:, None, :], jnp.sin(ay)[:, None, :]
    cz, sz = jnp.cos(az)[None], jnp.sin(az)[None]
    table = jnp.stack([cy * cz - sy * sz, -(sy * cz + cy * sz)])
    return table.reshape(2 * MY * MZ, ys * zs)


def x_tables(px, nx):
    kk = MX // px
    k = np.arange(MX).reshape(px, kk)
    phase = 2.0 * np.pi / nx * (k[:, :, None] * np.arange(nx) % nx)
    cosine, sine = np.cos(phase), np.sin(phase)
    table = np.zeros((2, px, GROUP, 2, kk, GROUP, nx))
    for c in range(GROUP):
        table[0, :, c, 0, :, c] = cosine
        table[0, :, c, 1, :, c] = -sine
        table[1, :, c, 0, :, c] = sine
        table[1, :, c, 1, :, c] = cosine
    table = table.reshape(2, 2 * MX * GROUP, GROUP * nx)
    high = table.astype(BF16)
    low = (table - high.astype(np.float64)).astype(BF16)
    return high, low


def dot(a, b):
    return jnp.dot(a, b, preferred_element_type=F32)


def cut(value):
    high = value.astype(BF16)
    return high, (value - high.astype(F32)).astype(BF16)


def dot3(a, high, low):
    ahigh, alow = cut(a)
    return dot(ahigh, high) + dot(alow, high) + dot(ahigh, low)


def to_modes(b0, b1, xh_ref, xl_ref):
    return dot3(b0, xh_ref[0], xl_ref[0]) + dot3(b1, xh_ref[1], xl_ref[1])


def store_modes(out_ref, group, value, px, py):
    wide = value.shape[1] // px
    tall = value.shape[0] // py
    for i in range(px):
        for j in range(py):
            out_ref[i * py + j, group] = value[j * tall : (j + 1) * tall, i * wide : (i + 1) * wide]


def build_fields(spec_ref, xh_ref, xl_ref, gh_ref, px, py):
    modes = MY * MZ
    for g in range(spec_ref.shape[1]):
        rows = []
        for j in range(py):
            rows.append(jnp.concatenate([spec_ref[i * py + j, g] for i in range(px)], axis=1))
        value = jnp.concatenate(rows, axis=0)
        for t in range(2):
            high = dot3(value, xh_ref[t], xl_ref[t]).astype(BF16)
            half = high.shape[1] // 2
            for h in range(2):
                gh_ref[2 * g + h, t * modes : (t + 1) * modes] = high[:, h * half : (h + 1) * half]


def pair_of(ref, start):
    chans, _, nx = ref.shape
    first = ref[:, pl.ds(start, SUB), :].reshape(chans * SUB, nx)
    second = ref[:, pl.ds(start + SUB, SUB), :].reshape(chans * SUB, nx)
    return jnp.concatenate([first, second], axis=1)


def channel_mix(kron_ref, in_ref, out_ref):
    chans, rows, nx = in_ref.shape

    def body(q, carry):
        start = pl.multiple_of(q * 2 * SUB, 2 * SUB)
        value = dot(kron_ref[...], pair_of(in_ref, start))
        out_ref[:, pl.ds(start, SUB), :] = value[:, :nx].reshape(chans, SUB, nx)
        out_ref[:, pl.ds(start + SUB, SUB), :] = value[:, nx:].reshape(chans, SUB, nx)
        return carry

    lax.fori_loop(0, rows // (2 * SUB), body, 0)


def position(py):
    return lax.axis_index("px") * py + lax.axis_index("py")


def partner(px, py, offset):
    other = lax.rem(position(py) + offset, px * py)
    return other, {"px": lax.div(other, py), "py": lax.rem(other, py)}


def greet(px, py):
    barrier = pltpu.get_barrier_semaphore()
    for offset in range(1, px * py):
        pl.semaphore_signal(
            barrier, inc=1, device_id=partner(px, py, offset)[1], device_id_type=pl.DeviceIdType.MESH
        )
    pl.semaphore_wait(barrier, px * py - 1)


def scatter_copy(px, py, offset, group, part_ref, land_ref, send_sem, recv_sem):
    other, device = partner(px, py, offset)
    return pltpu.make_async_remote_copy(
        part_ref.at[other, group], land_ref.at[offset, group], send_sem.at[offset, group], recv_sem.at[offset, group],
        device_id=device, device_id_type=pl.DeviceIdType.MESH,
    )


def scatter_kernel(px, py, part_ref, out_ref, land_ref, send_sem, recv_sem):
    count = px * py
    greet(px, py)
    groups = part_ref.shape[1]
    for g in range(groups):
        for offset in range(1, count):
            scatter_copy(px, py, offset, g, part_ref, land_ref, send_sem, recv_sem).start()
    out_ref[...] = part_ref[position(py)]
    for g in range(groups):
        for offset in range(1, count):
            scatter_copy(px, py, offset, g, part_ref, land_ref, send_sem, recv_sem).wait()
            out_ref[g] += land_ref[offset, g]


def gather_kernel(px, py, own_ref, out_ref, land_ref, send_sem, recv_sem):
    count = px * py
    greet(px, py)
    copies = []
    for offset in range(1, count):
        copies.append(
            pltpu.make_async_remote_copy(
                own_ref, land_ref.at[offset], send_sem.at[offset], recv_sem.at[offset],
                device_id=partner(px, py, offset)[1], device_id_type=pl.DeviceIdType.MESH,
            )
        )
        copies[-1].start()
    here = position(py)
    out_ref[here] = own_ref[...]
    for offset in range(1, count):
        copies[offset - 1].wait()
        out_ref[lax.rem(here + count - offset, count)] = land_ref[offset]


def mix_kernel(s_ref, w_ref, out_ref):
    chans = s_ref.shape[1]
    real = jnp.zeros(out_ref.shape[1:], F32)
    imag = jnp.zeros(out_ref.shape[1:], F32)
    for c in range(chans):
        s_real, s_imag = s_ref[0, c : c + 1], s_ref[1, c : c + 1]
        w_real, w_imag = w_ref[0, c].astype(F32), w_ref[1, c].astype(F32)
        real += s_real * w_real - s_imag * w_imag
        imag += s_real * w_imag + s_imag * w_real
    out_ref[0] = real
    out_ref[1] = imag


def adjoint_kernel(b_ref, w_ref, out_ref):
    b_real, b_imag = b_ref[0], b_ref[1]
    for c in range(w_ref.shape[1]):
        w_real, w_imag = w_ref[0, c].astype(F32), w_ref[1, c].astype(F32)
        out_ref[0, c : c + 1] = jnp.sum(b_real * w_real + b_imag * w_imag, axis=0, keepdims=True)
        out_ref[1, c : c + 1] = jnp.sum(b_imag * w_real - b_real * w_imag, axis=0, keepdims=True)


def forward_kernel(
    px, py, v_ref, th_ref, xh_ref, xl_ref, out_ref, part_ref, land_ref, send_sem, recv_sem
):
    modes = MY * MZ
    parts = []
    for p in range(GROUP // 2):
        value = jnp.concatenate([v_ref[2 * p], v_ref[2 * p + 1]], axis=1)
        parts.append(dot(th_ref[...], value))
    b0 = jnp.concatenate([part[:modes] for part in parts], axis=1)
    b1 = jnp.concatenate([part[modes:] for part in parts], axis=1)
    step = pl.program_id(0)
    store_modes(part_ref, step, to_modes(b0, b1, xh_ref, xl_ref), px, py)
    count = px * py

    @pl.when(step == 0)
    def _():
        greet(px, py)

    for offset in range(1, count):
        scatter_copy(px, py, offset, step, part_ref, land_ref, send_sem, recv_sem).start()

    @pl.when(step == pl.num_programs(0) - 1)
    def _():
        out_ref[...] = part_ref[position(py)]
        for g in range(part_ref.shape[1]):
            for offset in range(1, count):
                scatter_copy(px, py, offset, g, part_ref, land_ref, send_sem, recv_sem).wait()
                out_ref[g] += land_ref[offset, g]


def middle_kernel(
    px, py, steps, spec_ref, vb_ref, va_ref, ca_ref, uh_ref, th_ref, xh_ref, xl_ref, fh_ref, fl_ref,
    kron_ref, ia_ref, sl_ref, back_ref, point_ref, gh_ref, acc_ref, mix_ref,
):
    step = pl.program_id(0)
    modes = MY * MZ
    nx = vb_ref.shape[2]
    chans, rows = vb_ref.shape[:2]

    @pl.when(step == 0)
    def _():
        build_fields(spec_ref, xh_ref, xl_ref, gh_ref, px, py)
        acc_ref[...] = jnp.zeros_like(acc_ref)
        point_ref[...] = jnp.zeros_like(point_ref)

    channel_mix(kron_ref, vb_ref, mix_ref)
    c0 = math.sqrt(2.0 / math.pi)

    def body(p, carry):
        field = dot(uh_ref[...], gh_ref[p])
        slopes = []
        for h in range(2):
            d = 2 * p + h
            v = field[:, h * nx : (h + 1) * nx] + mix_ref[d]
            v2 = v * v
            t = jnp.tanh(v * (c0 + (c0 * 0.044715) * v2))
            half = 0.5 + 0.5 * t
            ia_ref[d] = (va_ref[d].astype(F32) - v * half).astype(BF16)
            deriv = half + (0.5 * v) * (1.0 - t * t) * (c0 + (3.0 * c0 * 0.044715) * v2)
            slope = (ca_ref[d].astype(F32) * deriv).astype(BF16)
            sl_ref[d] = slope
            slopes.append(slope)
        both = jnp.concatenate(slopes, axis=1)
        acc_ref[p] += dot(th_ref[...], both)
        return carry

    lax.fori_loop(0, chans // 2, body, 0)

    def point_body(q, carry):
        start = pl.multiple_of(q * 2 * SUB, 2 * SUB)
        point_ref[...] += lax.dot_general(
            pair_of(vb_ref, start), pair_of(sl_ref, start), (((1,), (1,)), ((), ())), preferred_element_type=F32
        )
        return carry

    lax.fori_loop(0, rows // (2 * SUB), point_body, 0)

    @pl.when(step == steps - 1)
    def _():
        for g in range(chans // GROUP):
            parts = [acc_ref[2 * g + h] for h in range(2)]
            b0 = jnp.concatenate([part[:modes] for part in parts], axis=1)
            b1 = jnp.concatenate([part[modes:] for part in parts], axis=1)
            store_modes(back_ref, g, to_modes(b0, b1, fh_ref, fl_ref), px, py)


def last_kernel(
    px, py, spec_ref, sl_ref, cb_ref, uh_ref, xh_ref, xl_ref, kron_ref, out_ref, gh_ref, mix_ref
):
    nx = sl_ref.shape[2]

    @pl.when(pl.program_id(0) == 0)
    def _():
        build_fields(spec_ref, xh_ref, xl_ref, gh_ref, px, py)

    channel_mix(kron_ref, sl_ref, mix_ref)

    def body(p, carry):
        field = dot(uh_ref[...], gh_ref[p])
        for h in range(2):
            d = 2 * p + h
            value = cb_ref[d].astype(F32) + field[:, h * nx : (h + 1) * nx] + mix_ref[d]
            out_ref[d] = value.astype(BF16)
        return carry

    lax.fori_loop(0, sl_ref.shape[0] // 2, body, 0)


def whole(shape):
    return pl.BlockSpec(shape, lambda i: (0,) * len(shape), pipeline_mode=pl.Buffered(1))


def per_device(state_a, state_b, cotan_a, cotan_b, spectral_weight, point_weight):
    samples, px, py = (lax.axis_size(name) for name in ("dp", "px", "py"))
    _, chans, ys, zs, nx = state_b.shape
    ny, nz = ys * px, zs * py
    cells, modes = ys * zs, MY * MZ
    groups = chans // GROUP
    kk = MX // px
    tall, wide = modes // py, 2 * MX * GROUP // px
    own = tall * kk
    scale_f = 1.0 / math.sqrt(nx * ny * nz)
    scale_i = 1.0 / math.sqrt(MX * MY * MZ)
    grad_scale = math.sqrt(MX * MY * MZ / (samples * nx * ny * nz))
    point_scale = 1.0 / math.sqrt(samples * nx * ny * nz)
    shape = (ys, zs, ny, nz)
    th = analysis_table(shape).astype(BF16)
    uh = synthesis_table(shape).astype(BF16)
    xh, xl = x_tables(px, nx)
    fh, fl = (jnp.asarray(np.ascontiguousarray(table.transpose(0, 2, 1))) for table in (xh, xl))
    xh, xl = jnp.asarray(xh), jnp.asarray(xl)
    eye = jnp.eye(SUB, dtype=BF16)
    kron_f = (point_weight.T[:, None, :, None] * eye[None, :, None, :]).reshape(chans * SUB, chans * SUB)
    kron_b = (point_weight[:, None, :, None] * eye[None, :, None, :]).reshape(chans * SUB, chans * SUB)
    field_a, field_b, cot_a, cot_b = (
        value.reshape(chans, cells, nx) for value in (state_a, state_b, cotan_a, cotan_b)
    )
    part_shape = jax.ShapeDtypeStruct((px * py, groups, tall, wide), F32)
    params = pltpu.CompilerParams(vmem_limit_bytes=LIMIT)

    count = px * py
    own_shape = jax.ShapeDtypeStruct((groups, tall, wide), F32)
    exchange = [
        pltpu.VMEM(part_shape.shape, F32),
        pltpu.SemaphoreType.DMA((count, groups)),
        pltpu.SemaphoreType.DMA((count, groups)),
    ]

    def linked(number):
        return pltpu.CompilerParams(vmem_limit_bytes=LIMIT, collective_id=number, has_side_effects=True)

    def to_channels(value):
        value = value.reshape(groups, tall, GROUP, 2, kk).transpose(3, 0, 2, 1, 4)
        return value.reshape(2, chans, own)

    def gather(value, number):
        value = value.reshape(2, groups, GROUP, tall, kk).transpose(1, 3, 2, 0, 4)
        value = value.reshape(groups, tall, wide)
        return pl.pallas_call(
            lambda *refs: gather_kernel(px, py, *refs),
            in_specs=[pl.BlockSpec(memory_space=pltpu.VMEM)],
            out_specs=pl.BlockSpec(memory_space=pltpu.VMEM),
            out_shape=part_shape,
            scratch_shapes=[
                pltpu.VMEM(part_shape.shape, F32), pltpu.SemaphoreType.DMA((count,)), pltpu.SemaphoreType.DMA((count,)),
            ],
            compiler_params=linked(number),
            interpret=INTERPRET,
            name="gather",
        )(value)

    def mode_product(kernel, value, name):
        return pl.pallas_call(
            kernel,
            out_shape=jax.ShapeDtypeStruct((2, chans, own), F32),
            compiler_params=params,
            interpret=INTERPRET,
            name=name,
        )(value, weight)

    spectrum = pl.pallas_call(
        lambda *refs: forward_kernel(px, py, *refs),
        grid=(groups,),
        in_specs=[
            pl.BlockSpec((GROUP, cells, nx), lambda i: (i, 0, 0)),
            whole(th.shape), whole(fh.shape), whole(fl.shape),
        ],
        out_specs=whole(own_shape.shape),
        out_shape=own_shape,
        scratch_shapes=[pltpu.VMEM(part_shape.shape, F32)] + exchange,
        compiler_params=linked(0),
        interpret=INTERPRET,
        name="forward",
    )(field_b, th, fh, fl)
    weight = spectral_weight.transpose(3, 4, 5, 0, 1, 2).reshape(2, chans, chans, own)
    spectrum = to_channels(spectrum) * scale_f
    mixed = gather(mode_product(mix_kernel, spectrum, "mix") * scale_i, 1)

    rows = min(256, cells)
    steps = cells // rows
    block = pl.BlockSpec((chans, rows, nx), lambda i: (0, i, 0))
    u_block = pl.BlockSpec((rows, 2 * modes), lambda i: (i, 0))
    t_block = pl.BlockSpec((2 * modes, rows), lambda i: (0, i))
    field_shape = jax.ShapeDtypeStruct((chans, cells, nx), BF16)
    side = chans * SUB
    g_scratch = [pltpu.VMEM((chans // 2, 2 * modes, 2 * nx), BF16)]
    input_a, slope, back_part, point = pl.pallas_call(
        lambda *refs: middle_kernel(px, py, steps, *refs),
        grid=(steps,),
        in_specs=[
            whole(part_shape.shape), block, block, block, u_block, t_block,
            whole(xh.shape), whole(xl.shape), whole(fh.shape), whole(fl.shape), whole((side, side)),
        ],
        out_specs=[block, block, whole(part_shape.shape), whole((side, side))],
        out_shape=[field_shape, field_shape, part_shape, jax.ShapeDtypeStruct((side, side), F32)],
        scratch_shapes=g_scratch
        + [pltpu.VMEM((chans // 2, 2 * modes, 2 * nx), F32), pltpu.VMEM((chans, rows, nx), F32)],
        compiler_params=params,
        interpret=INTERPRET,
        name="middle",
    )(mixed, field_b, field_a, cot_a, uh, th, xh, xl, fh, fl, kron_f)

    back = pl.pallas_call(
        lambda *refs: scatter_kernel(px, py, *refs),
        in_specs=[pl.BlockSpec(memory_space=pltpu.VMEM)],
        out_specs=pl.BlockSpec(memory_space=pltpu.VMEM),
        out_shape=own_shape,
        scratch_shapes=exchange,
        compiler_params=linked(2),
        interpret=INTERPRET,
        name="scatter",
    )(back_part)
    back = to_channels(back) * scale_i
    grad_spec = gather(mode_product(adjoint_kernel, back, "adjoint") * scale_f, 3)
    grad_b = pl.pallas_call(
        lambda *refs: last_kernel(px, py, *refs),
        grid=(steps,),
        in_specs=[
            whole(part_shape.shape), block, block, u_block,
            whole(xh.shape), whole(xl.shape), whole((side, side)),
        ],
        out_specs=block,
        out_shape=field_shape,
        scratch_shapes=g_scratch + [pltpu.VMEM((chans, rows, nx), F32)],
        compiler_params=params,
        interpret=INTERPRET,
        name="last",
    )(grad_spec, slope, cot_b, uh, xh, xl, kron_b)

    share = chans // samples
    spec_all = lax.all_gather(spectrum, "dp", axis=0)
    back_all = lax.all_gather(back, "dp", axis=0)
    back_own = lax.dynamic_slice_in_dim(back_all, lax.axis_index("dp") * share, share, axis=2)
    p_real, p_imag = spec_all[:, 0, :, None], spec_all[:, 1, :, None]
    q_real, q_imag = back_own[:, 0, None], back_own[:, 1, None]
    grad_real = jnp.sum(p_real * q_real + p_imag * q_imag, axis=0)
    grad_imag = jnp.sum(p_real * q_imag - p_imag * q_real, axis=0)
    grad = jnp.stack([grad_real, grad_imag]) * grad_scale
    spectral_grad = grad.reshape(2, chans, share, tall // MZ, MZ, kk).transpose(3, 4, 5, 0, 1, 2)

    point = jnp.sum(point.reshape(chans, SUB, chans, SUB) * jnp.eye(SUB, dtype=F32)[None, :, None, :], axis=(1, 3))
    point_total = lax.psum(point, ("dp", "px", "py")) * point_scale
    full = state_b.shape
    return (input_a.reshape(full), grad_b.reshape(full), spectral_grad, point_total)


def solution(mesh):
    return jax.shard_map(
        per_device,
        mesh=mesh,
        in_specs=(
            P("dp", None, "px", "py", None),
            P("dp", None, "px", "py", None),
            P("dp", None, "px", "py", None),
            P("dp", None, "px", "py", None),
            P("py", None, "px", None, None, None),
            P(),
        ),
        out_specs=(
            P("dp", None, "px", "py", None),
            P("dp", None, "px", "py", None),
            P("py", None, "px", None, None, "dp"),
            P(),
        ),
        check_vma=False,
    )
```
